512 devices in a mesh: row: 16 (over z), col: 32 (over y, x, core).
Axes of the slice: x: 4, y: 4, z: 16, core: 2. Of those that a mesh axis runs over, the one named last changes fastest.
Arguments:
- vertices: float32 [3, 61440], P(None, ('row', 'col')), may hold values from -6 to 6
- connect: int32 [4, 61440], P(None, ('row', 'col')), may hold values from 0 to 119
- component: int32 [61440], P(('row', 'col')), may hold values from 0 to 4
- azimuth: float32 [1], replicated, may hold values from 0 to 6.2831
- adjoint_rhs: float32 [24, 61440], P(None, ('row', 'col')), may hold values from -6 to 6
Outputs:
- solution: float32 [24, 61440], P(None, ('row', 'col'))
- residual_sq: float32 [24], replicated
The draws below stay inside these ranges and needn't reach their ends.
Inputs may be any that keep to these rules, and one draw needn't show every extreme that they name: Entry connect[k, p] names vertex (p // 120) * 120 + connect[k, p], a vertex of the panel's own block. `component`: 0 marks a panel of the airframe body, b > 0 a panel of blade b.
All inputs are finite; a program needn't handle non-finite values.
Results may differ from the reference program's by a relative error of at most 0.0003.
Values sent between devices are 32-bit elements; how exact they have to be, the bound alone decides.
No kernel may reach another device: no remote copies, remote signals or barrier semaphores. Data moves between devices by JAX's collectives and lax.ppermute only.
A program may use at most 64 MiB of HBM per device.

```python
import math
import jax
import jax.numpy as jnp
from jax import lax

UNIT = 120
RHS = 24
BLADES = 4
ORDER = 61440


def set_ends(drawn, key, low, largest):
    longest = drawn.shape.index(max(drawn.shape))
    spots = []
    for shift in (0, 1):
        where = [jax.random.randint(jax.random.fold_in(key, axis), (), 0, length) for axis, length in enumerate(drawn.shape)]
        where[longest] = (where[longest] + shift) % drawn.shape[longest]
        spots.append(tuple(where))
    return drawn.at[spots[0]].set(low).at[spots[1]].set(largest)


def block_levels(stream_key, extent, pieces, least, largest):
    def one(axis_at, parts):
        steps = jax.random.uniform(jax.random.fold_in(jax.random.fold_in(stream_key, 6), axis_at), (parts,), jnp.float32, least / len(pieces), largest / len(pieces))
        return jnp.repeat(jnp.exp(steps), extent[axis_at] // parts).reshape((-1,) + (1,) * (len(extent) - axis_at - 1))

    gain = one(*pieces[0])
    for cut in pieces[1:]:
        gain = gain * one(*cut)
    return gain


def gaussian(stream_key, shape, width, reach, pieces=(), held_as=jnp.bfloat16):
    drawn = width * jax.random.normal(stream_key, shape, jnp.float32)
    if pieces:
        drawn = drawn * block_levels(stream_key, shape, pieces, -0.22, 0.18)
    return jnp.clip(drawn, -reach, reach).astype(held_as)


def setup_inputs(seed: int = 0) -> dict:
    key_list = jax.random.split(jax.random.key(seed), 6)
    vertices = gaussian(key_list[0], (3, ORDER), 1.0, 6.0, ((1, 512),), jnp.float32)
    connect = set_ends(jax.random.randint(key_list[1], (4, ORDER), 0, UNIT), jax.random.fold_in(key_list[1], 1), 0, UNIT - 1).astype(jnp.int32)
    component = set_ends(jax.random.randint(key_list[2], (ORDER,), 0, BLADES + 1), jax.random.fold_in(key_list[2], 1), 0, BLADES).astype(jnp.int32)
    azimuth = jnp.clip(jax.random.uniform(key_list[3], (1,), jnp.float32, 0.0, 6.2831), 0.0, 6.2831)
    adjoint_rhs = gaussian(key_list[4], (RHS, ORDER), 1.0, 6.0, ((1, 512),), jnp.float32)
    return {"vertices": vertices, "connect": connect, "component": component, "azimuth": azimuth, "adjoint_rhs": adjoint_rhs}


epsilon = 1e-06
core_square = 0.04
highest = lax.Precision.HIGHEST

def panel_frame(corners, component, azimuth, blades):
    angle_turn = azimuth[0] + 2.0 * math.pi / blades * (component - 1).astype(jnp.float32)
    cosine = jnp.cos(angle_turn)[None, :]
    sine_turn = jnp.sin(angle_turn)[None, :]
    on_rotor = (component > 0)[None, :]
    xcoord = corners[0]
    ycoord = corners[1]
    turned_x = jnp.where(on_rotor, cosine * xcoord - sine_turn * ycoord, xcoord)
    turned_y = jnp.where(on_rotor, sine_turn * xcoord + cosine * ycoord, ycoord)
    placed = jnp.stack([turned_x, turned_y, corners[2]])
    centers = lax.optimization_barrier(jnp.mean(placed, axis=1))
    diagonal_one = placed[:, 2] - placed[:, 0]
    diagonal_two = placed[:, 3] - placed[:, 1]
    areas = 0.5 * jnp.stack([diagonal_one[1] * diagonal_two[2] - diagonal_one[2] * diagonal_two[1], diagonal_one[2] * diagonal_two[0] - diagonal_one[0] * diagonal_two[2], diagonal_one[0] * diagonal_two[1] - diagonal_one[1] * diagonal_two[0]])
    return jnp.concatenate([centers, areas], axis=0)

def influence(receivers, sources, scale):
    delta_x = receivers[0][:, None] - sources[0][None, :]
    delta_y = receivers[1][:, None] - sources[1][None, :]
    delta_z = receivers[2][:, None] - sources[2][None, :]
    inverse = lax.rsqrt(delta_x * delta_x + delta_y * delta_y + delta_z * delta_z + core_square)
    doublet = (sources[3][None, :] * delta_x + sources[4][None, :] * delta_y + sources[5][None, :] * delta_z) * (inverse * inverse * inverse)
    return scale * (doublet + sources[5][None, :] * inverse)

def small_solve(start_norm, first_diag, first_sub, second_top, second_diag, second_sub):
    det_value = second_sub * second_sub * (first_diag * first_diag + first_sub * first_sub) + (first_diag * second_diag - first_sub * second_top) ** 2
    gram_00 = first_diag * first_diag + first_sub * first_sub
    gram_01 = first_diag * second_top + first_sub * second_diag
    gram_11 = second_top * second_top + second_diag * second_diag + second_sub * second_sub
    coef_one = start_norm * (gram_11 * first_diag - gram_01 * second_top) / det_value
    coef_two = start_norm * (gram_00 * second_top - gram_01 * first_diag) / det_value
    error_one = start_norm - first_diag * coef_one - second_top * coef_two
    error_two = -first_sub * coef_one - second_diag * coef_two
    error_three = -second_sub * coef_two
    return (coef_one, coef_two, error_one * error_one + error_two * error_two + error_three * error_three)

def reference(vertices, connect, component, azimuth, adjoint_rhs):
    order = vertices.shape[1]
    panel = jnp.arange(order, dtype=jnp.int32)
    base_index = panel // UNIT * UNIT
    corners = vertices[:, (base_index[None, :] + connect).astype(jnp.int32)]
    frames = panel_frame(corners, component, azimuth, BLADES)
    diag_term = 3.0 + jnp.sqrt(lax.optimization_barrier(jnp.sum(frames[3:] * frames[3:], axis=0)))
    scale = 2.0 / math.sqrt(order)
    block_rows = UNIT * 4
    block_count = order // block_rows

    def apply_matrix(vector):

        def step_block(block_index, total):
            begin = (block_index * block_rows).astype(jnp.int32)
            receivers = lax.dynamic_slice_in_dim(frames, begin, block_rows, 1)
            piece = lax.dynamic_slice_in_dim(vector, begin, block_rows, 1)
            return total + jnp.dot(piece, influence(receivers, frames, scale), precision=highest, preferred_element_type=jnp.float32)
        summed = lax.fori_loop(0, block_count, step_block, jnp.zeros(vector.shape, jnp.float32))
        return summed + diag_term[None, :] * vector
    rhs_value = adjoint_rhs
    start_norm = jnp.sqrt(lax.optimization_barrier(jnp.sum(rhs_value * rhs_value, axis=1)) + epsilon)
    basis_one = rhs_value / start_norm[:, None]
    image_one = apply_matrix(basis_one)
    first_diag = lax.optimization_barrier(jnp.sum(basis_one * image_one, axis=1))
    ortho_one = image_one - first_diag[:, None] * basis_one
    first_sub = jnp.sqrt(lax.optimization_barrier(jnp.sum(ortho_one * ortho_one, axis=1)) + epsilon)
    basis_two = ortho_one / first_sub[:, None]
    image_two = apply_matrix(basis_two)
    second_top = lax.optimization_barrier(jnp.sum(basis_one * image_two, axis=1))
    second_diag = lax.optimization_barrier(jnp.sum(basis_two * image_two, axis=1))
    ortho_two = image_two - second_top[:, None] * basis_one - second_diag[:, None] * basis_two
    second_sub = jnp.sqrt(lax.optimization_barrier(jnp.sum(ortho_two * ortho_two, axis=1)) + epsilon)
    coef_one, coef_two, residual_sq = small_solve(start_norm, first_diag, first_sub, second_top, second_diag, second_sub)
    solution = coef_one[:, None] * basis_one + coef_two[:, None] * basis_two
    return (solution, residual_sq)
```

```python
import math

import jax
import jax.numpy as jnp
from jax import lax
from jax.sharding import PartitionSpec as P

BLADES = 4


epsilon = 1e-06
core_square = 0.04
highest = lax.Precision.HIGHEST


def panel_frame(corners, component, azimuth, blades):
    angle_turn = azimuth[0] + 2.0 * math.pi / blades * (component - 1).astype(jnp.float32)
    cosine = jnp.cos(angle_turn)[None, :]
    sine_turn = jnp.sin(angle_turn)[None, :]
    on_rotor = (component > 0)[None, :]
    xcoord = corners[0]
    ycoord = corners[1]
    turned_x = jnp.where(on_rotor, cosine * xcoord - sine_turn * ycoord, xcoord)
    turned_y = jnp.where(on_rotor, sine_turn * xcoord + cosine * ycoord, ycoord)
    placed = jnp.stack([turned_x, turned_y, corners[2]])
    centers = jnp.mean(placed, axis=1)
    diagonal_one = placed[:, 2] - placed[:, 0]
    diagonal_two = placed[:, 3] - placed[:, 1]
    areas = 0.5 * jnp.stack(
        [
            diagonal_one[1] * diagonal_two[2] - diagonal_one[2] * diagonal_two[1],
            diagonal_one[2] * diagonal_two[0] - diagonal_one[0] * diagonal_two[2],
            diagonal_one[0] * diagonal_two[1] - diagonal_one[1] * diagonal_two[0],
        ]
    )
    return jnp.concatenate([centers, areas], axis=0)


def influence(receivers, sources, scale):
    delta_x = receivers[0][:, None] - sources[0][None, :]
    delta_y = receivers[1][:, None] - sources[1][None, :]
    delta_z = receivers[2][:, None] - sources[2][None, :]
    inverse = lax.rsqrt(delta_x * delta_x + delta_y * delta_y + delta_z * delta_z + core_square)
    doublet = (
        sources[3][None, :] * delta_x
        + sources[4][None, :] * delta_y
        + sources[5][None, :] * delta_z
    ) * (inverse * inverse * inverse)
    return scale * (doublet + sources[5][None, :] * inverse)


def small_solve(start_norm, first_diag, first_sub, second_top, second_diag, second_sub):
    det_value = (
        second_sub * second_sub * (first_diag * first_diag + first_sub * first_sub)
        + (first_diag * second_diag - first_sub * second_top) ** 2
    )
    gram_00 = first_diag * first_diag + first_sub * first_sub
    gram_01 = first_diag * second_top + first_sub * second_diag
    gram_11 = second_top * second_top + second_diag * second_diag + second_sub * second_sub
    coef_one = start_norm * (gram_11 * first_diag - gram_01 * second_top) / det_value
    coef_two = start_norm * (gram_00 * second_top - gram_01 * first_diag) / det_value
    error_one = start_norm - first_diag * coef_one - second_top * coef_two
    error_two = -first_sub * coef_one - second_diag * coef_two
    error_three = -second_sub * coef_two
    return (
        coef_one,
        coef_two,
        error_one * error_one + error_two * error_two + error_three * error_three,
    )


def spread(value, axis):
    size = lax.axis_size(axis)
    return lax.all_to_all(jnp.broadcast_to(value[None], (size,) + value.shape), axis, 0, 0)


def on_device(vertices, connect, component, azimuth, adjoint_rhs):
    width = vertices.shape[1]
    rows, cols = lax.axis_size("row"), lax.axis_size("col")
    rhs = adjoint_rhs.shape[0]
    scale = 2.0 / math.sqrt(width * rows * cols)
    lookup = (connect[:, :, None] == jnp.arange(width, dtype=jnp.int32)[None, None, :]).astype(
        jnp.float32
    )
    corners = jnp.einsum("cv,kpv->ckp", vertices, lookup, precision=highest)
    frames = panel_frame(corners, component, azimuth, BLADES)
    area_size = jnp.sqrt(jnp.sum(frames[3:] * frames[3:], axis=0))
    sources = spread(frames, "col").transpose(1, 0, 2).reshape(6, cols * width)
    received = spread(jnp.concatenate([frames[:3], adjoint_rhs], axis=0), "row")
    received = received.transpose(1, 0, 2).reshape(3 + rhs, rows * width)
    receivers = received[:3]

    def apply_matrix(own, gathered):
        partial_sums = jnp.dot(
            gathered,
            influence(receivers, sources, scale),
            precision=highest,
            preferred_element_type=jnp.float32,
        )
        pieces = partial_sums.reshape(rhs, cols, width).transpose(1, 0, 2)
        summed = jnp.sum(lax.all_to_all(pieces, "col", 0, 0), axis=0)
        return summed + area_size[None, :] * own

    power_zero = adjoint_rhs
    power_one = apply_matrix(power_zero, received[3:])
    gathered = spread(power_one, "row").transpose(1, 0, 2).reshape(rhs, rows * width)
    power_two = apply_matrix(power_one, gathered)

    def inner(left, right):
        return jnp.sum(left * right, axis=1)

    gram = jnp.stack(
        [
            inner(power_zero, power_zero),
            inner(power_zero, power_one),
            inner(power_zero, power_two),
            inner(power_one, power_one),
            inner(power_one, power_two),
            inner(power_two, power_two),
        ]
    )
    gram = jnp.sum(spread(gram, "col"), axis=0)
    gram = jnp.sum(spread(gram, "row"), axis=0)
    g00, g01, g02, g11, g12, g22 = gram
    norm_square = g00 + epsilon
    start_norm = jnp.sqrt(norm_square)
    alpha = (g01 - 3.0 * epsilon) / norm_square
    first_diag = 3.0 + alpha
    sub_square = jnp.maximum(g11 - 2.0 * alpha * g01 + alpha * alpha * g00, 0.0) / norm_square
    first_square = sub_square + epsilon
    first_sub = jnp.sqrt(first_square)
    second_top = (3.0 * (g01 - alpha * g00) + (g02 - alpha * g01)) / (norm_square * first_sub)
    unit_two = sub_square / first_square
    quotient = (g12 - alpha * (g11 + g02) + alpha * alpha * g01) / (norm_square * first_square)
    second_diag = 3.0 * unit_two + quotient
    beta = second_diag - 3.0
    on_one = -(alpha + beta)
    on_zero = alpha * beta - second_top * first_sub
    last_square = (
        g22
        + on_one * on_one * g11
        + on_zero * on_zero * g00
        + 2.0 * (on_one * g12 + on_zero * g02 + on_one * on_zero * g01)
    ) / (norm_square * first_square)
    second_sub = jnp.sqrt(jnp.maximum(last_square, 0.0) + epsilon)
    coef_one, coef_two, residual_sq = small_solve(
        start_norm, first_diag, first_sub, second_top, second_diag, second_sub
    )
    from_one = coef_two / (start_norm * first_sub)
    from_zero = coef_one / start_norm - alpha * from_one
    solution = from_zero[:, None] * power_zero + from_one[:, None] * power_one
    return (solution, residual_sq)


def solution(mesh):
    in_specs = (
        P(None, ("row", "col")),
        P(None, ("row", "col")),
        P(("row", "col")),
        P(),
        P(None, ("row", "col")),
    )
    out_specs = (P(None, ("row", "col")), P())
    return jax.shard_map(
        on_device, mesh=mesh, in_specs=in_specs, out_specs=out_specs, check_vma=False
    )
```
